32 devices in a mesh: grp: 8 (over z, core), rep: 4 (over y, x).
Axes of the slice: x: 2, y: 2, z: 4, core: 2. Of those that a mesh axis runs over, the one named last changes fastest.
Arguments:
- queries: bfloat16 [12288, 2560], P(('grp', 'rep')), may hold values from -60 to 60
- passages: bfloat16 [65536, 2560], P(('grp', 'rep')), may hold values from -60 to 60
- block_valid_counts: int32 [512], P(('grp', 'rep')), may hold values from 16 to 128
- positive_index: int32 [12288], P(('grp', 'rep')), may hold values from 0 to 2047, as said below
- neg_blocks: int32 [32, 12], P(('grp', 'rep')), may hold values from 0 to 511, as said below
- query_weights: float32 [12288], P(('grp', 'rep')), may hold values from 0.3 to 10
Outputs:
- query_loss: float32 [12288], P(('grp', 'rep'))
- mean_loss: float32 [], replicated
The draws below stay inside these ranges and needn't reach their ends.
Inputs may be any that keep to these rules, and one draw needn't show every extreme that they name: `neg_blocks`: row g lists 12 distinct blocks, all owned by query groups with the same rep index as group g and another grp index; at most 2 of them belong to one group, and some group gives exactly 2 in every row. `positive_index`: always a valid row of one of the query's own group's blocks.
All inputs are finite; a program needn't handle non-finite values.
Results may differ from the reference program's by a relative error of at most 0.0003.
Values may be sent and summed in bfloat16 or wider, within the bound.
A program may use at most 256 MiB of HBM per device.

```python
import jax
import jax.numpy as jnp
from jax import lax

D = 2560
QG = 384
BPD = 16
BR = 128
CAP = 2
NEG = 12
QUERIES = 12288
NBLOCKS = 512
PASSAGES = 65536
N_GRP = 8
N_REP = 4


cluster_count = 32


def cluster_rows(key, rows, salt):
    centers = jax.random.normal(jax.random.fold_in(key, 101), (cluster_count, D), jnp.float32)
    column_scale = jnp.exp(jax.random.uniform(jax.random.fold_in(key, 102), (D,), jnp.float32, -1.15, 1.15))
    own_key = jax.random.fold_in(key, salt)
    key_labels, target_length_factor, key_noise = jax.random.split(own_key, 3)
    labels = jax.random.randint(key_labels, (rows,), 0, cluster_count)
    row_scale = jnp.exp(jax.random.uniform(target_length_factor, (rows, 1), jnp.float32, -1.15, 1.15))
    noise = jax.random.normal(key_noise, (rows, D), jnp.float32)
    member = jnp.take(centers, labels, axis=0)
    return jnp.clip(row_scale * (member + noise * column_scale), -60.0, 60.0)


def draw_queries(key, part):
    return cluster_rows(key, QUERIES, 7).astype(jnp.bfloat16)


def draw_passages(key, part):
    return cluster_rows(key, PASSAGES, 9).astype(jnp.bfloat16)


def counts_helper(key):
    return jax.random.randint(jax.random.fold_in(key, 11), (NBLOCKS,), BR // 8, BR + 1).astype(jnp.int32)


def draw_block_valid_counts(key, part):
    return counts_helper(key)


def draw_positive_index(key, part):
    counts = counts_helper(key)
    key_block, key_row = jax.random.split(jax.random.fold_in(key, 13), 2)
    chosen = jax.random.randint(key_block, (QUERIES,), 0, BPD)
    device = jnp.arange(QUERIES, dtype=jnp.int32) // QG
    top_row = counts[device * BPD + chosen]
    row = jax.random.randint(key_row, (QUERIES,), 0, top_row)
    return (chosen * BR + row).astype(jnp.int32)


def draw_neg_blocks(key, part):

    def per_device(device_key, device):
        group = device // N_REP
        replica = device % N_REP
        key_order, key_slot_positions, key_local, key_shuffle = jax.random.split(device_key, 4)
        others = jnp.arange(N_GRP - 1, dtype=jnp.int32)
        others = others + (others >= group).astype(jnp.int32)
        order = jax.random.permutation(key_order, others)
        chosen_slots = jax.random.permutation(key_slot_positions, (N_GRP - 2) * CAP)[:NEG - CAP]
        owner_group = jnp.concatenate([jnp.full((CAP,), order[0], jnp.int32), order[1:][chosen_slots // CAP]])
        slot_rank = jnp.concatenate([jnp.arange(CAP, dtype=jnp.int32), (chosen_slots % CAP).astype(jnp.int32)])
        local_table = jax.vmap(lambda sub_key: jax.random.permutation(sub_key, BPD))(jax.random.split(key_local, N_GRP))
        local_block = local_table[owner_group, slot_rank]
        global_block = (owner_group * N_REP + replica) * BPD + local_block
        return jax.random.permutation(key_shuffle, global_block).astype(jnp.int32)
    device_keys = jax.random.split(jax.random.fold_in(key, 17), N_GRP * N_REP)
    return jax.vmap(per_device)(device_keys, jnp.arange(N_GRP * N_REP, dtype=jnp.int32))


def draw_query_weights(key, part):
    position = jnp.arange(QUERIES, dtype=jnp.float32)
    ramp = 1.0 + 2.0 * position / (QUERIES - 1)
    base = jnp.exp(jax.random.uniform(jax.random.fold_in(key, 19), (QUERIES,), jnp.float32, -1.2, 1.2))
    return base * ramp


def setup_inputs(seed: int = 0) -> dict:
    streams_of = jax.random.split(jax.random.key(seed), 7)
    return {
        "queries": draw_queries(jax.random.fold_in(streams_of[6], 71), 0),
        "passages": draw_passages(jax.random.fold_in(streams_of[6], 71), 0),
        "block_valid_counts": draw_block_valid_counts(jax.random.fold_in(streams_of[6], 71), 0),
        "positive_index": draw_positive_index(jax.random.fold_in(streams_of[6], 71), 0),
        "neg_blocks": draw_neg_blocks(jax.random.fold_in(streams_of[6], 71), 0),
        "query_weights": draw_query_weights(jax.random.fold_in(streams_of[6], 71), 0),
    }


inverse_softmax_sharpness = 20.0
norm_epsilon = 1e-06

def normalize(rows):
    values = rows.astype(jnp.float32)
    scale = lax.rsqrt(lax.optimization_barrier(jnp.sum(values * values, axis=-1, keepdims=True)) + norm_epsilon)
    return (values * scale).astype(jnp.bfloat16)

def reference(queries, passages, block_valid_counts, positive_index, neg_blocks, query_weights):
    local_rows = BPD * BR
    all_blocks = passages.reshape(NBLOCKS, BR, D)

    def per_device(device):
        question_unit_vectors = normalize(lax.dynamic_slice_in_dim(queries, device * QG, QG, 0))
        document_unit_vectors = normalize(lax.dynamic_slice_in_dim(passages, device * local_rows, local_rows, 0))
        own_counts = lax.dynamic_slice_in_dim(block_valid_counts, device * BPD, BPD, 0)
        row_valid = jnp.arange(local_rows, dtype=jnp.int32) % BR < jnp.repeat(own_counts, BR)
        shared_pool_similarity = jnp.dot(question_unit_vectors, document_unit_vectors.T, preferred_element_type=jnp.float32) * inverse_softmax_sharpness
        local_total = lax.optimization_barrier(jnp.sum(jnp.where(row_valid[None, :], jnp.exp(shared_pool_similarity), 0.0), axis=1))
        positives = lax.dynamic_slice_in_dim(positive_index, device * QG, QG, 0)
        positive_score = jnp.take_along_axis(shared_pool_similarity, positives[:, None], axis=1)[:, 0]
        wanted = neg_blocks[device]
        distractor_unit_vectors = normalize(all_blocks[wanted]).reshape(NEG * BR, D)
        hard_valid = jnp.arange(NEG * BR, dtype=jnp.int32) % BR < jnp.repeat(block_valid_counts[wanted], BR)
        distractor_similarity = jnp.dot(question_unit_vectors, distractor_unit_vectors.T, preferred_element_type=jnp.float32) * inverse_softmax_sharpness
        hard_total = lax.optimization_barrier(jnp.sum(jnp.where(hard_valid[None, :], jnp.exp(distractor_similarity), 0.0), axis=1))
        return jnp.log(local_total + hard_total) - positive_score
    query_loss = lax.map(per_device, jnp.arange(N_GRP * N_REP, dtype=jnp.int32)).reshape(QUERIES)
    mean_loss = jnp.sum(query_weights * query_loss) / jnp.sum(query_weights)
    return (query_loss, mean_loss)
```

```python
import functools

import jax
import jax.numpy as jnp
from jax import lax
from jax.experimental import pallas as pl
from jax.experimental.pallas import tpu as pltpu
from jax.sharding import PartitionSpec as P

sharpness = 20.0
norm_epsilon = 1e-06
LANES = 128
MESH = pl.DeviceIdType.MESH


def unit(rows):
    values = rows.astype(jnp.float32)
    scale = lax.rsqrt(jnp.sum(values * values, axis=-1, keepdims=True) + norm_epsilon)
    return (values * scale).astype(jnp.bfloat16)


def scores(passage_rows, query_rows):
    return (
        lax.dot_general(
            passage_rows,
            query_rows,
            (((1,), (1,)), ((), ())),
            preferred_element_type=jnp.float32,
        )
        * sharpness
    )


def kernel(
    G,
    REP,
    counts,
    neg,
    positive,
    weights,
    q_hbm,
    p_hbm,
    loss_ref,
    mean_ref,
    qall,
    pun,
    qown,
    qsub,
    wants_out,
    wants_in,
    wants_s,
    table,
    tot_out,
    tot_in,
    part_out,
    part_grp,
    sum_out,
    part_rep,
    q_sem,
    p_sem,
    want_send,
    want_recv,
    smem_sem,
    right_send,
    left_send,
    side_send,
    recv,
    tot_send,
    tot_recv,
    grp_send,
    grp_recv,
    rep_send,
    rep_recv,
):
    g = lax.axis_index("grp")
    r = lax.axis_index("rep")
    blocks, BR, D = p_hbm.shape
    QG = q_hbm.shape[0]
    listed = neg.shape[1]
    R = LANES
    NS = QG // R
    C = G // 2
    z = g // 2
    c = g % 2
    side = 2 * z + 1 - c

    barrier = pltpu.get_barrier_semaphore()
    for k in range(1, G):
        pl.semaphore_signal(
            barrier, inc=1, device_id={"grp": lax.rem(g + k, G)}, device_id_type=MESH
        )
    for k in range(1, REP):
        pl.semaphore_signal(
            barrier, inc=1, device_id={"rep": lax.rem(r + k, REP)}, device_id_type=MESH
        )

    own_copy = pltpu.make_async_copy(q_hbm, qown, q_sem)
    own_copy.start()

    def passage_copy(b):
        return pltpu.make_async_copy(p_hbm.at[b], pun.at[b], p_sem.at[b])

    @pl.loop(0, blocks)
    def _(b):
        passage_copy(b).start()

    wants_out[...] = jnp.zeros_like(wants_out)
    wants_out[0:1, 0:listed] = neg[...]
    pl.semaphore_wait(barrier, G - 1 + REP - 1)

    def want_copy(k):
        return pltpu.make_async_remote_copy(
            wants_out,
            wants_in.at[g],
            want_send.at[k],
            want_recv.at[g],
            device_id={"grp": lax.rem(g + k, G)},
            device_id_type=MESH,
        )

    def want_arrival(k):
        src = lax.rem(g + k, G)
        return pltpu.make_async_remote_copy(
            wants_out,
            wants_in.at[src],
            want_send.at[k],
            want_recv.at[src],
            device_id={"grp": src},
            device_id_type=MESH,
        )

    def own_piece(j, sem, target):
        rows = pl.ds(pl.multiple_of(j * R, R), R)
        return pltpu.make_async_remote_copy(
            q_hbm.at[rows],
            qall.at[g, rows],
            sem.at[g, j],
            recv.at[g, j],
            device_id={"grp": target},
            device_id_type=MESH,
        )

    def piece(gq, j, sem, target):
        rows = pl.ds(pl.multiple_of(j * R, R), R)
        return pltpu.make_async_remote_copy(
            qall.at[gq, rows],
            qall.at[gq, rows],
            sem.at[gq, j],
            recv.at[gq, j],
            device_id={"grp": target},
            device_id_type=MESH,
        )

    for k in range(1, G):
        want_copy(k).start()

    @pl.loop(0, NS)
    def _(j):
        @pl.when(z + 1 < C)
        def _():
            own_piece(j, right_send, g + 2).start()

        @pl.when(z > 0)
        def _():
            own_piece(j, left_send, g - 2).start()

        own_piece(j, side_send, side).start()

    own_copy.wait()

    @pl.loop(0, NS)
    def _(j):
        rows = pl.ds(pl.multiple_of(j * R, R), R)
        qown[rows, :] = unit(qown[rows, :])

    def own_block(b, carry):
        total, pos = carry
        passage_copy(b).wait()
        pun[b] = unit(pun[b])
        st = scores(pun[b], qown[...])
        row = lax.broadcasted_iota(jnp.int32, st.shape, 0)
        live = row < counts[b]
        total = total + jnp.sum(jnp.where(live, jnp.exp(st), 0.0), axis=0, keepdims=True)
        hit = row + b * BR == positive[...]
        pos = pos + jnp.sum(jnp.where(hit, st, 0.0), axis=0, keepdims=True)
        return total, pos

    zero = jnp.zeros((1, QG), jnp.float32)
    local_total, pos = lax.fori_loop(0, blocks, own_block, (zero, zero))
    tot_in[g, 0:1, :] = local_total

    for k in range(1, G):
        want_arrival(k).wait_recv()
    wants_in[g] = wants_out[...]
    to_smem = pltpu.make_async_copy(wants_in, wants_s, smem_sem)
    to_smem.start()
    to_smem.wait()
    me = g * REP + r

    @pl.loop(0, G)
    def _(gq):
        found = jnp.int32(0)
        first = jnp.int32(0)
        second = jnp.int32(0)
        for i in range(listed):
            w = wants_s[gq, 0, i]
            local = w - me * blocks
            mine = jnp.logical_and(local >= 0, local < blocks)
            first = jnp.where(jnp.logical_and(mine, found == 0), local, first)
            second = jnp.where(jnp.logical_and(mine, found == 1), local, second)
            found = found + mine.astype(jnp.int32)
        table[gq, 0] = first
        table[gq, 1] = jnp.where(found > 0, counts[first], 0)
        table[gq, 2] = second
        table[gq, 3] = jnp.where(found > 1, counts[second], 0)

    def tot_copy(gq):
        return pltpu.make_async_remote_copy(
            tot_out.at[gq],
            tot_in.at[g],
            tot_send.at[gq],
            tot_recv.at[g],
            device_id={"grp": gq},
            device_id_type=MESH,
        )

    def tot_arrival(src):
        return pltpu.make_async_remote_copy(
            tot_out.at[src],
            tot_in.at[src],
            tot_send.at[src],
            tot_recv.at[src],
            device_id={"grp": src},
            device_id_type=MESH,
        )

    def hard(gq, j):
        rows = pl.ds(pl.multiple_of(j * R, R), R)
        qsub[...] = unit(qall[gq, rows, :])
        total = jnp.zeros((1, R), jnp.float32)
        for slot in range(2):
            st = scores(pun[table[gq, 2 * slot]], qsub[...])
            row = lax.broadcasted_iota(jnp.int32, st.shape, 0)
            live = row < table[gq, 2 * slot + 1]
            total = total + jnp.sum(jnp.where(live, jnp.exp(st), 0.0), axis=0, keepdims=True)
        tot_out[gq, 0:1, rows] = total

        @pl.when(j == NS - 1)
        def _():
            tot_copy(gq).start()

    def step(e, carry):
        s = e // NS
        j = e % NS
        left = z - s
        right = z + s
        from_left = jnp.logical_and(s > 0, left >= 0)
        from_right = jnp.logical_and(s > 0, right < C)

        @pl.when(from_left)
        def _():
            gq = 2 * left + c
            piece(gq, j, right_send, g).wait_recv()

            @pl.when(z + 1 < C)
            def _():
                piece(gq, j, right_send, g + 2).start()

            piece(gq, j, side_send, side).start()

        @pl.when(from_right)
        def _():
            gq = 2 * right + c
            piece(gq, j, left_send, g).wait_recv()

            @pl.when(z > 0)
            def _():
                piece(gq, j, left_send, g - 2).start()

            piece(gq, j, side_send, side).start()

        @pl.loop(0, 4)
        def _(t):
            zq = jnp.where(t % 2 == 0, left, right)
            cq = jnp.where(t < 2, c, 1 - c)
            there = jnp.where(t % 2 == 0, left >= 0, jnp.logical_and(s > 0, right < C))
            there = jnp.logical_and(there, jnp.logical_or(s > 0, t >= 2))
            gq = 2 * zq + cq

            @pl.when(there)
            def _():
                @pl.when(t >= 2)
                def _():
                    piece(gq, j, side_send, g).wait_recv()

                hard(gq, j)

        return carry

    lax.fori_loop(0, C * NS, step, 0)

    for k in range(1, G):
        tot_arrival(lax.rem(g + k, G)).wait_recv()
    total = tot_in[0, 0:1, :]
    for k in range(1, G):
        total = total + tot_in[k, 0:1, :]
    loss = jnp.log(total) - pos
    loss_ref[...] = loss
    w = weights[...]
    lane = lax.broadcasted_iota(jnp.int32, (8, LANES), 1)
    weighted = jnp.sum(w * loss, axis=1, keepdims=True)
    weight = jnp.sum(w, axis=1, keepdims=True)
    part = jnp.where(lane == 0, weighted, jnp.where(lane == 1, weight, 0.0))

    def exchange(axis, me_, n, out, slots, send, rec):
        def copy(k):
            return pltpu.make_async_remote_copy(
                out,
                slots.at[me_],
                send.at[k],
                rec.at[me_],
                device_id={axis: lax.rem(me_ + k, n)},
                device_id_type=MESH,
            )

        def arrival(k):
            src = lax.rem(me_ + k, n)
            return pltpu.make_async_remote_copy(
                out,
                slots.at[src],
                send.at[k],
                rec.at[src],
                device_id={axis: src},
                device_id_type=MESH,
            )

        for k in range(1, n):
            copy(k).start()
        for k in range(1, n):
            arrival(k).wait_recv()
        for k in range(1, n):
            copy(k).wait_send()

    part_out[...] = part
    part_grp[g] = part
    exchange("grp", g, G, part_out, part_grp, grp_send, grp_recv)
    total = part_grp[0]
    for k in range(1, G):
        total = total + part_grp[k]
    sum_out[...] = total
    part_rep[r] = total
    exchange("rep", r, REP, sum_out, part_rep, rep_send, rep_recv)
    total = part_rep[0]
    for k in range(1, REP):
        total = total + part_rep[k]
    mean_ref[...] = jnp.broadcast_to(total[:, 0:1] / total[:, 1:2], mean_ref.shape)

    for k in range(1, G):
        want_copy(k).wait_send()
        tot_copy(lax.rem(g + k, G)).wait_send()

    @pl.loop(0, NS)
    def _(j):
        @pl.when(z + 1 < C)
        def _():
            own_piece(j, right_send, g + 2).wait_send()

        @pl.when(z > 0)
        def _():
            own_piece(j, left_send, g - 2).wait_send()

        own_piece(j, side_send, side).wait_send()

    @pl.loop(NS, C * NS)
    def _(e):
        s = e // NS
        j = e % NS
        left = z - s
        right = z + s

        @pl.when(left >= 0)
        def _():
            gq = 2 * left + c

            @pl.when(z + 1 < C)
            def _():
                piece(gq, j, right_send, g + 2).wait_send()

            piece(gq, j, side_send, side).wait_send()

        @pl.when(right < C)
        def _():
            gq = 2 * right + c

            @pl.when(z > 0)
            def _():
                piece(gq, j, left_send, g - 2).wait_send()

            piece(gq, j, side_send, side).wait_send()


def local(G, REP, queries, passages, counts, positive, neg, weights):
    QG, D = queries.shape
    blocks = counts.shape[0]
    BR = passages.shape[0] // blocks
    NS = QG // LANES
    dma = pltpu.SemaphoreType.DMA
    vmem = pl.BlockSpec(memory_space=pltpu.VMEM)
    smem = pl.BlockSpec(memory_space=pltpu.SMEM)
    hbm = pl.BlockSpec(memory_space=pl.ANY)
    loss, mean = pl.pallas_call(
        functools.partial(kernel, G, REP),
        out_shape=(
            jax.ShapeDtypeStruct((1, QG), jnp.float32),
            jax.ShapeDtypeStruct((8, LANES), jnp.float32),
        ),
        in_specs=[smem, vmem, vmem, vmem, hbm, hbm],
        out_specs=(vmem, vmem),
        scratch_shapes=[
            pltpu.VMEM((G, QG, D), jnp.bfloat16),
            pltpu.VMEM((blocks, BR, D), jnp.bfloat16),
            pltpu.VMEM((QG, D), jnp.bfloat16),
            pltpu.VMEM((LANES, D), jnp.bfloat16),
            pltpu.VMEM((8, LANES), jnp.int32),
            pltpu.VMEM((G, 8, LANES), jnp.int32),
            pltpu.SMEM((G, 8, LANES), jnp.int32),
            pltpu.SMEM((G, 4), jnp.int32),
            pltpu.VMEM((G, 8, QG), jnp.float32),
            pltpu.VMEM((G, 8, QG), jnp.float32),
            pltpu.VMEM((8, LANES), jnp.float32),
            pltpu.VMEM((G, 8, LANES), jnp.float32),
            pltpu.VMEM((8, LANES), jnp.float32),
            pltpu.VMEM((REP, 8, LANES), jnp.float32),
            dma,
            dma((blocks,)),
            dma((G,)),
            dma((G,)),
            dma,
            dma((G, NS)),
            dma((G, NS)),
            dma((G, NS)),
            dma((G, NS)),
            dma((G,)),
            dma((G,)),
            dma((G,)),
            dma((G,)),
            dma((REP,)),
            dma((REP,)),
        ],
        compiler_params=pltpu.CompilerParams(
            collective_id=0, has_side_effects=True, vmem_limit_bytes=62 * 1024 * 1024
        ),
    )(
        counts,
        neg,
        positive.reshape(1, QG),
        weights.reshape(1, QG),
        queries,
        passages.reshape(blocks, BR, D),
    )
    return loss.reshape(QG), mean[0, 0]


def solution(mesh):
    split = P(("grp", "rep"))
    rows = P(("grp", "rep"), None)
    return jax.shard_map(
        functools.partial(local, mesh.shape["grp"], mesh.shape["rep"]),
        mesh=mesh,
        in_specs=(rows, rows, split, split, rows, split),
        out_specs=(split, P()),
        check_vma=False,
    )
```

```python
import functools

import jax
import jax.numpy as jnp
from jax import lax
from jax.experimental import pallas as pl
from jax.experimental.pallas import tpu as pltpu
from jax.sharding import PartitionSpec as P

sharpness = 20.0
norm_epsilon = 1e-06
LANES = 128
MESH = pl.DeviceIdType.MESH


def unit(rows):
    values = rows.astype(jnp.float32)
    scale = lax.rsqrt(jnp.sum(values * values, axis=-1, keepdims=True) + norm_epsilon)
    return (values * scale).astype(jnp.bfloat16)


def scores(passage_rows, query_rows):
    return (
        lax.dot_general(
            passage_rows,
            query_rows,
            (((1,), (1,)), ((), ())),
            preferred_element_type=jnp.float32,
        )
        * sharpness
    )


def kernel(
    G,
    REP,
    counts,
    neg,
    positive,
    weights,
    q_hbm,
    p_hbm,
    loss_ref,
    mean_ref,
    qall,
    pun,
    qown,
    qsub,
    wants_out,
    wants_in,
    wants_s,
    table,
    tot_out,
    tot_in,
    part_out,
    part_grp,
    sum_out,
    part_rep,
    blk_out,
    blk_in,
    live_out,
    live_in,
    q_sem,
    p_sem,
    want_send,
    want_recv,
    smem_sem,
    right_send,
    left_send,
    side_send,
    recv,
    tot_send,
    tot_recv,
    grp_send,
    grp_recv,
    rep_send,
    rep_recv,
    blk_send,
    blk_recv,
    live_send,
    live_recv,
):
    g = lax.axis_index("grp")
    r = lax.axis_index("rep")
    blocks, BR, D = p_hbm.shape
    QG = q_hbm.shape[0]
    listed = neg.shape[1]
    R = LANES
    NS = QG // R
    C = G // 2
    z = g // 2
    c = g % 2
    side = 2 * z + 1 - c

    short = C >= 4

    def by_blocks(owner_z, query_z):
        if not short:
            return owner_z < 0
        return jnp.logical_or(
            jnp.logical_and(owner_z == 0, query_z == 1),
            jnp.logical_and(owner_z == C - 1, query_z == C - 2),
        )

    inner_z = jnp.where(z == 0, 1, C - 2)
    end_z = jnp.where(z == 1, 0, C - 1)
    at_end = by_blocks(z, inner_z)
    by_end = by_blocks(end_z, z)
    own_right = jnp.logical_and(z + 1 < C, jnp.logical_not(by_blocks(z + 1, z)))
    own_left = jnp.logical_and(z > 0, jnp.logical_not(by_blocks(z - 1, z)))

    barrier = pltpu.get_barrier_semaphore()
    for k in range(1, G):
        pl.semaphore_signal(
            barrier, inc=1, device_id={"grp": lax.rem(g + k, G)}, device_id_type=MESH
        )
    for k in range(1, REP):
        pl.semaphore_signal(
            barrier, inc=1, device_id={"rep": lax.rem(r + k, REP)}, device_id_type=MESH
        )

    own_copy = pltpu.make_async_copy(q_hbm, qown, q_sem)
    own_copy.start()

    def passage_copy(b):
        return pltpu.make_async_copy(p_hbm.at[b], pun.at[b], p_sem.at[b])

    @pl.loop(0, blocks)
    def _(b):
        passage_copy(b).start()

    wants_out[...] = jnp.zeros_like(wants_out)
    wants_out[0:1, 0:listed] = neg[...]
    pl.semaphore_wait(barrier, G - 1 + REP - 1)

    def want_copy(k):
        return pltpu.make_async_remote_copy(
            wants_out,
            wants_in.at[g],
            want_send.at[k],
            want_recv.at[g],
            device_id={"grp": lax.rem(g + k, G)},
            device_id_type=MESH,
        )

    def want_arrival(k):
        src = lax.rem(g + k, G)
        return pltpu.make_async_remote_copy(
            wants_out,
            wants_in.at[src],
            want_send.at[k],
            want_recv.at[src],
            device_id={"grp": src},
            device_id_type=MESH,
        )

    def own_piece(j, sem, target):
        rows = pl.ds(pl.multiple_of(j * R, R), R)
        return pltpu.make_async_remote_copy(
            q_hbm.at[rows],
            qall.at[g, rows],
            sem.at[g, j],
            recv.at[g, j],
            device_id={"grp": target},
            device_id_type=MESH,
        )

    def piece(gq, j, sem, target):
        rows = pl.ds(pl.multiple_of(j * R, R), R)
        return pltpu.make_async_remote_copy(
            qall.at[gq, rows],
            qall.at[gq, rows],
            sem.at[gq, j],
            recv.at[gq, j],
            device_id={"grp": target},
            device_id_type=MESH,
        )

    for k in range(1, G):
        want_copy(k).start()

    @pl.loop(0, NS)
    def _(j):
        @pl.when(own_right)
        def _():
            own_piece(j, right_send, g + 2).start()

        @pl.when(own_left)
        def _():
            own_piece(j, left_send, g - 2).start()

        own_piece(j, side_send, side).start()

    own_copy.wait()

    @pl.loop(0, NS)
    def _(j):
        rows = pl.ds(pl.multiple_of(j * R, R), R)
        qown[rows, :] = unit(qown[rows, :])

    def own_block(b, carry):
        total, pos = carry
        passage_copy(b).wait()
        pun[b] = unit(pun[b])
        st = scores(pun[b], qown[...])
        row = lax.broadcasted_iota(jnp.int32, st.shape, 0)
        live = row < counts[b]
        total = total + jnp.sum(jnp.where(live, jnp.exp(st), 0.0), axis=0, keepdims=True)
        hit = row + b * BR == positive[...]
        pos = pos + jnp.sum(jnp.where(hit, st, 0.0), axis=0, keepdims=True)
        return total, pos

    zero = jnp.zeros((1, QG), jnp.float32)
    local_total, pos = lax.fori_loop(0, blocks, own_block, (zero, zero))
    tot_in[g, 0:1, :] = local_total

    for k in range(1, G):
        want_arrival(k).wait_recv()
    wants_in[g] = wants_out[...]
    to_smem = pltpu.make_async_copy(wants_in, wants_s, smem_sem)
    to_smem.start()
    to_smem.wait()
    me = g * REP + r

    @pl.loop(0, G)
    def _(gq):
        found = jnp.int32(0)
        first = jnp.int32(0)
        second = jnp.int32(0)
        for i in range(listed):
            w = wants_s[gq, 0, i]
            local = w - me * blocks
            mine = jnp.logical_and(local >= 0, local < blocks)
            first = jnp.where(jnp.logical_and(mine, found == 0), local, first)
            second = jnp.where(jnp.logical_and(mine, found == 1), local, second)
            found = found + mine.astype(jnp.int32)
        table[gq, 0] = first
        table[gq, 1] = jnp.where(found > 0, counts[first], 0)
        table[gq, 2] = second
        table[gq, 3] = jnp.where(found > 1, counts[second], 0)

    def blk_copy(t):
        slot = t // 2
        cq = t % 2
        return pltpu.make_async_remote_copy(
            blk_out.at[cq, slot],
            blk_in.at[c, slot],
            blk_send.at[cq, slot],
            blk_recv.at[c, slot],
            device_id={"grp": 2 * inner_z + cq},
            device_id_type=MESH,
        )

    def live_copy(cq):
        return pltpu.make_async_remote_copy(
            live_out.at[cq],
            live_in.at[c],
            live_send.at[cq],
            live_recv.at[c],
            device_id={"grp": 2 * inner_z + cq},
            device_id_type=MESH,
        )

    def blk_arrival(t):
        slot = t // 2
        co = t % 2
        return pltpu.make_async_remote_copy(
            blk_out.at[co, slot],
            blk_in.at[co, slot],
            blk_send.at[co, slot],
            blk_recv.at[co, slot],
            device_id={"grp": 2 * end_z + co},
            device_id_type=MESH,
        )

    def live_arrival(co):
        return pltpu.make_async_remote_copy(
            live_out.at[co],
            live_in.at[co],
            live_send.at[co],
            live_recv.at[co],
            device_id={"grp": 2 * end_z + co},
            device_id_type=MESH,
        )

    @pl.when(at_end)
    def _():
        @pl.loop(0, 4)
        def _(t):
            slot = t // 2
            cq = t % 2
            gq = 2 * inner_z + cq
            blk_out[cq, slot] = pun[table[gq, 2 * slot]]
            live_out[cq, slot] = jnp.full((8, QG), table[gq, 2 * slot + 1], jnp.int32)

        @pl.loop(0, 2)
        def _(cq):
            live_copy(cq).start()

        @pl.loop(0, 4)
        def _(t):
            blk_copy(t).start()

    def tot_copy(gq):
        return pltpu.make_async_remote_copy(
            tot_out.at[gq],
            tot_in.at[g],
            tot_send.at[gq],
            tot_recv.at[g],
            device_id={"grp": gq},
            device_id_type=MESH,
        )

    def tot_arrival(src):
        return pltpu.make_async_remote_copy(
            tot_out.at[src],
            tot_in.at[src],
            tot_send.at[src],
            tot_recv.at[src],
            device_id={"grp": src},
            device_id_type=MESH,
        )

    def hard(gq, j):
        rows = pl.ds(pl.multiple_of(j * R, R), R)
        qsub[...] = unit(qall[gq, rows, :])
        total = jnp.zeros((1, R), jnp.float32)
        for slot in range(2):
            st = scores(pun[table[gq, 2 * slot]], qsub[...])
            row = lax.broadcasted_iota(jnp.int32, st.shape, 0)
            live = row < table[gq, 2 * slot + 1]
            total = total + jnp.sum(jnp.where(live, jnp.exp(st), 0.0), axis=0, keepdims=True)
        tot_out[gq, 0:1, rows] = total

        @pl.when(j == NS - 1)
        def _():
            tot_copy(gq).start()

    def sources(e):
        s = e // NS
        left = z - s
        right = z + s
        from_left = jnp.logical_and(left >= 0, jnp.logical_not(by_blocks(z, left)))
        from_right = jnp.logical_and(right < C, jnp.logical_not(by_blocks(z, right)))
        return s, e % NS, left, right, from_left, from_right

    def forward(e):
        s, j, left, right, from_left, from_right = sources(e)

        @pl.when(from_left)
        def _():
            gq = 2 * left + c
            piece(gq, j, right_send, g).wait_recv()

            @pl.when(z + 1 < C)
            def _():
                piece(gq, j, right_send, g + 2).start()

            piece(gq, j, side_send, side).start()

        @pl.when(from_right)
        def _():
            gq = 2 * right + c
            piece(gq, j, left_send, g).wait_recv()

            @pl.when(z > 0)
            def _():
                piece(gq, j, left_send, g - 2).start()

            piece(gq, j, side_send, side).start()

    @pl.loop(0, C * NS)
    def _(e):
        if C > 1:

            @pl.when(jnp.logical_or(e == 0, e > NS))
            def _():
                forward(jnp.where(e == 0, NS, e))

        s, j, left, right, from_left, from_right = sources(e)

        @pl.loop(0, 4)
        def _(t):
            is_left = t % 2 == 0
            zq = jnp.where(is_left, left, right)
            cq = jnp.where(t < 2, c, 1 - c)
            there = jnp.logical_or(
                jnp.logical_and(is_left, from_left),
                jnp.logical_and(jnp.logical_and(t % 2 == 1, s > 0), from_right),
            )
            there = jnp.logical_and(there, jnp.logical_or(s > 0, t >= 2))
            gq = 2 * zq + cq

            @pl.when(there)
            def _():
                @pl.when(t >= 2)
                def _():
                    piece(gq, j, side_send, g).wait_recv()

                hard(gq, j)

    @pl.when(by_end)
    def _():
        @pl.loop(0, 2)
        def _(co):
            live_arrival(co).wait_recv()
            tot_in[2 * end_z + co] = jnp.zeros((8, QG), jnp.float32)

        @pl.loop(0, 4)
        def _(t):
            slot = t // 2
            co = t % 2
            blk_arrival(t).wait_recv()
            st = scores(blk_in[co, slot], qown[...])
            row = lax.broadcasted_iota(jnp.int32, st.shape, 0)
            live = row < live_in[co, slot, 0:1, :]
            tot_in[2 * end_z + co, 0:1, :] += jnp.sum(
                jnp.where(live, jnp.exp(st), 0.0), axis=0, keepdims=True
            )

    @pl.loop(1, G)
    def _(k):
        src = lax.rem(g + k, G)

        @pl.when(jnp.logical_not(by_blocks(src // 2, z)))
        def _():
            tot_arrival(src).wait_recv()

    total = tot_in[0, 0:1, :]
    for k in range(1, G):
        total = total + tot_in[k, 0:1, :]
    loss = jnp.log(total) - pos
    loss_ref[...] = loss
    w = weights[...]
    lane = lax.broadcasted_iota(jnp.int32, (8, LANES), 1)
    weighted = jnp.sum(w * loss, axis=1, keepdims=True)
    weight = jnp.sum(w, axis=1, keepdims=True)
    part = jnp.where(lane == 0, weighted, jnp.where(lane == 1, weight, 0.0))

    def exchange(axis, me_, n, out, slots, send, rec):
        def copy(k):
            return pltpu.make_async_remote_copy(
                out,
                slots.at[me_],
                send.at[k],
                rec.at[me_],
                device_id={axis: lax.rem(me_ + k, n)},
                device_id_type=MESH,
            )

        def arrival(k):
            src = lax.rem(me_ + k, n)
            return pltpu.make_async_remote_copy(
                out,
                slots.at[src],
                send.at[k],
                rec.at[src],
                device_id={axis: src},
                device_id_type=MESH,
            )

        for k in range(1, n):
            copy(k).start()
        for k in range(1, n):
            arrival(k).wait_recv()
        for k in range(1, n):
            copy(k).wait_send()

    part_out[...] = part
    part_grp[g] = part
    exchange("grp", g, G, part_out, part_grp, grp_send, grp_recv)
    total = part_grp[0]
    for k in range(1, G):
        total = total + part_grp[k]
    sum_out[...] = total
    part_rep[r] = total
    exchange("rep", r, REP, sum_out, part_rep, rep_send, rep_recv)
    total = part_rep[0]
    for k in range(1, REP):
        total = total + part_rep[k]
    mean_ref[...] = jnp.broadcast_to(total[:, 0:1] / total[:, 1:2], mean_ref.shape)

    for k in range(1, G):
        want_copy(k).wait_send()

    @pl.loop(1, G)
    def _(k):
        dst = lax.rem(g + k, G)

        @pl.when(jnp.logical_not(by_blocks(z, dst // 2)))
        def _():
            tot_copy(dst).wait_send()

    @pl.when(at_end)
    def _():
        @pl.loop(0, 2)
        def _(cq):
            live_copy(cq).wait_send()

        @pl.loop(0, 4)
        def _(t):
            blk_copy(t).wait_send()

    @pl.loop(0, NS)
    def _(j):
        @pl.when(own_right)
        def _():
            own_piece(j, right_send, g + 2).wait_send()

        @pl.when(own_left)
        def _():
            own_piece(j, left_send, g - 2).wait_send()

        own_piece(j, side_send, side).wait_send()

    @pl.loop(NS, C * NS)
    def _(e):
        _, j, left, right, from_left, from_right = sources(e)

        @pl.when(from_left)
        def _():
            gq = 2 * left + c

            @pl.when(z + 1 < C)
            def _():
                piece(gq, j, right_send, g + 2).wait_send()

            piece(gq, j, side_send, side).wait_send()

        @pl.when(from_right)
        def _():
            gq = 2 * right + c

            @pl.when(z > 0)
            def _():
                piece(gq, j, left_send, g - 2).wait_send()

            piece(gq, j, side_send, side).wait_send()


def local(G, REP, queries, passages, counts, positive, neg, weights):
    QG, D = queries.shape
    blocks = counts.shape[0]
    BR = passages.shape[0] // blocks
    NS = QG // LANES
    dma = pltpu.SemaphoreType.DMA
    vmem = pl.BlockSpec(memory_space=pltpu.VMEM)
    smem = pl.BlockSpec(memory_space=pltpu.SMEM)
    hbm = pl.BlockSpec(memory_space=pl.ANY)
    loss, mean = pl.pallas_call(
        functools.partial(kernel, G, REP),
        out_shape=(
            jax.ShapeDtypeStruct((1, QG), jnp.float32),
            jax.ShapeDtypeStruct((8, LANES), jnp.float32),
        ),
        in_specs=[smem, vmem, vmem, vmem, hbm, hbm],
        out_specs=(vmem, vmem),
        scratch_shapes=[
            pltpu.VMEM((G, QG, D), jnp.bfloat16),
            pltpu.VMEM((blocks, BR, D), jnp.bfloat16),
            pltpu.VMEM((QG, D), jnp.bfloat16),
            pltpu.VMEM((LANES, D), jnp.bfloat16),
            pltpu.VMEM((8, LANES), jnp.int32),
            pltpu.VMEM((G, 8, LANES), jnp.int32),
            pltpu.SMEM((G, 8, LANES), jnp.int32),
            pltpu.SMEM((G, 4), jnp.int32),
            pltpu.VMEM((G, 8, QG), jnp.float32),
            pltpu.VMEM((G, 8, QG), jnp.float32),
            pltpu.VMEM((8, LANES), jnp.float32),
            pltpu.VMEM((G, 8, LANES), jnp.float32),
            pltpu.VMEM((8, LANES), jnp.float32),
            pltpu.VMEM((REP, 8, LANES), jnp.float32),
            pltpu.VMEM((2, 2, BR, D), jnp.bfloat16),
            pltpu.VMEM((2, 2, BR, D), jnp.bfloat16),
            pltpu.VMEM((2, 2, 8, QG), jnp.int32),
            pltpu.VMEM((2, 2, 8, QG), jnp.int32),
            dma,
            dma((blocks,)),
            dma((G,)),
            dma((G,)),
            dma,
            dma((G, NS)),
            dma((G, NS)),
            dma((G, NS)),
            dma((G, NS)),
            dma((G,)),
            dma((G,)),
            dma((G,)),
            dma((G,)),
            dma((REP,)),
            dma((REP,)),
            dma((2, 2)),
            dma((2, 2)),
            dma((2,)),
            dma((2,)),
        ],
        compiler_params=pltpu.CompilerParams(
            collective_id=0, has_side_effects=True, vmem_limit_bytes=62 * 1024 * 1024
        ),
    )(
        counts,
        neg,
        positive.reshape(1, QG),
        weights.reshape(1, QG),
        queries,
        passages.reshape(blocks, BR, D),
    )
    return loss.reshape(QG), mean[0, 0]


def solution(mesh):
    split = P(("grp", "rep"))
    rows = P(("grp", "rep"), None)
    return jax.shard_map(
        functools.partial(local, mesh.shape["grp"], mesh.shape["rep"]),
        mesh=mesh,
        in_specs=(rows, rows, split, split, rows, split),
        out_specs=(split, P()),
        check_vma=False,
    )
```

```python
import functools

import jax
import jax.numpy as jnp
from jax import lax
from jax.experimental import pallas as pl
from jax.experimental.pallas import tpu as pltpu
from jax.sharding import PartitionSpec as P

sharpness = 20.0
norm_epsilon = 1e-06
LANES = 128
PIECE = 64
WINDOW = 2
MESH = pl.DeviceIdType.MESH


def unit(rows):
    values = rows.astype(jnp.float32)
    scale = lax.rsqrt(jnp.sum(values * values, axis=-1, keepdims=True) + norm_epsilon)
    return (values * scale).astype(jnp.bfloat16)


def scores(passage_rows, query_rows):
    return (
        lax.dot_general(
            passage_rows,
            query_rows,
            (((1,), (1,)), ((), ())),
            preferred_element_type=jnp.float32,
        )
        * sharpness
    )


def kernel(
    G,
    REP,
    counts,
    neg,
    positive,
    weights,
    q_hbm,
    p_hbm,
    loss_ref,
    mean_ref,
    qall,
    pun,
    qown,
    qsub,
    wants_out,
    wants_in,
    wants_s,
    table,
    tot_out,
    tot_in,
    part_out,
    part_grp,
    sum_out,
    part_rep,
    blk_out,
    blk_in,
    live_out,
    live_in,
    q_sem,
    p_sem,
    want_send,
    want_recv,
    smem_sem,
    right_send,
    left_send,
    side_send,
    recv,
    tot_send,
    tot_recv,
    grp_send,
    grp_recv,
    rep_send,
    rep_recv,
    blk_send,
    blk_recv,
    live_send,
    live_recv,
):
    g = lax.axis_index("grp")
    r = lax.axis_index("rep")
    blocks, BR, D = p_hbm.shape
    QG = q_hbm.shape[0]
    listed = neg.shape[1]
    R = LANES
    NS = QG // R
    T = PIECE if R % PIECE == 0 else R
    NT = QG // T
    per = R // T
    W = min(WINDOW, NT)
    C = G // 2
    z = g // 2
    c = g % 2
    side = 2 * z + 1 - c

    short = C >= 4

    def by_blocks(owner_z, query_z):
        if not short:
            return owner_z < 0
        return jnp.logical_or(
            jnp.logical_and(owner_z == 0, query_z == 1),
            jnp.logical_and(owner_z == C - 1, query_z == C - 2),
        )

    inner_z = jnp.where(z == 0, 1, C - 2)
    end_z = jnp.where(z == 1, 0, C - 1)
    at_end = by_blocks(z, inner_z)
    by_end = by_blocks(end_z, z)
    own_right = jnp.logical_and(z + 1 < C, jnp.logical_not(by_blocks(z + 1, z)))
    own_left = jnp.logical_and(z > 0, jnp.logical_not(by_blocks(z - 1, z)))

    barrier = pltpu.get_barrier_semaphore()
    for k in range(1, G):
        pl.semaphore_signal(
            barrier, inc=1, device_id={"grp": lax.rem(g + k, G)}, device_id_type=MESH
        )
    for k in range(1, REP):
        pl.semaphore_signal(
            barrier, inc=1, device_id={"rep": lax.rem(r + k, REP)}, device_id_type=MESH
        )

    own_copy = pltpu.make_async_copy(q_hbm, qown, q_sem)
    own_copy.start()

    def passage_copy(b):
        return pltpu.make_async_copy(p_hbm.at[b], pun.at[b], p_sem.at[b])

    @pl.loop(0, blocks)
    def _(b):
        passage_copy(b).start()

    wants_out[...] = jnp.zeros_like(wants_out)
    wants_out[0:1, 0:listed] = neg[...]
    pl.semaphore_wait(barrier, G - 1 + REP - 1)

    def want_copy(k):
        return pltpu.make_async_remote_copy(
            wants_out,
            wants_in.at[g],
            want_send.at[k],
            want_recv.at[g],
            device_id={"grp": lax.rem(g + k, G)},
            device_id_type=MESH,
        )

    def want_arrival(k):
        src = lax.rem(g + k, G)
        return pltpu.make_async_remote_copy(
            wants_out,
            wants_in.at[src],
            want_send.at[k],
            want_recv.at[src],
            device_id={"grp": src},
            device_id_type=MESH,
        )

    def own_piece(j, sem, target):
        rows = pl.ds(pl.multiple_of(j * T, T), T)
        return pltpu.make_async_remote_copy(
            q_hbm.at[rows],
            qall.at[g, rows],
            sem.at[g, j],
            recv.at[g, j],
            device_id={"grp": target},
            device_id_type=MESH,
        )

    def piece(gq, j, sem, target):
        rows = pl.ds(pl.multiple_of(j * T, T), T)
        return pltpu.make_async_remote_copy(
            qall.at[gq, rows],
            qall.at[gq, rows],
            sem.at[gq, j],
            recv.at[gq, j],
            device_id={"grp": target},
            device_id_type=MESH,
        )

    for k in range(1, G):
        want_copy(k).start()

    right_skip = jnp.where(own_right, W, NT)
    left_skip = jnp.where(own_left, W, NT)

    def comes_from_left(e):
        left = z - e // NT
        return jnp.logical_and(
            e >= NT, jnp.logical_and(left >= 0, jnp.logical_not(by_blocks(z, left)))
        )

    def comes_from_right(e):
        right = z + e // NT
        return jnp.logical_and(
            e >= NT, jnp.logical_and(right < C, jnp.logical_not(by_blocks(z, right)))
        )

    def goes_right(e):
        own = jnp.logical_and(own_right, jnp.logical_and(e >= 0, e < NT))
        return jnp.logical_or(own, jnp.logical_and(z + 1 < C, comes_from_left(e)))

    def goes_left(e):
        own = jnp.logical_and(own_left, jnp.logical_and(e >= 0, e < NT))
        return jnp.logical_or(own, jnp.logical_and(z > 0, comes_from_right(e)))

    def right_sent(e):
        @pl.when(goes_right(e))
        def _():
            piece(2 * (z - e // NT) + c, e % NT, right_send, g + 2).wait_send()

    def left_sent(e):
        @pl.when(goes_left(e))
        def _():
            piece(2 * (z + e // NT) + c, e % NT, left_send, g - 2).wait_send()

    def send_own(n):
        @pl.when(own_right)
        def _():
            own_piece(n, right_send, g + 2).start()

        @pl.when(own_left)
        def _():
            own_piece(n, left_send, g - 2).start()

    def move_right(n):
        e = n + right_skip

        @pl.when(jnp.logical_and(own_right, e < NT))
        def _():
            right_sent(e - W)
            own_piece(e, right_send, g + 2).start()

        @pl.when(comes_from_left(e))
        def _():
            gq = 2 * (z - e // NT) + c
            j = e % NT
            piece(gq, j, right_send, g).wait_recv()

            @pl.when(z + 1 < C)
            def _():
                right_sent(e - W)
                piece(gq, j, right_send, g + 2).start()

            piece(gq, j, side_send, side).start()

    def move_left(n):
        e = n + left_skip

        @pl.when(jnp.logical_and(own_left, e < NT))
        def _():
            left_sent(e - W)
            own_piece(e, left_send, g - 2).start()

        @pl.when(comes_from_right(e))
        def _():
            gq = 2 * (z + e // NT) + c
            j = e % NT
            piece(gq, j, left_send, g).wait_recv()

            @pl.when(z > 0)
            def _():
                left_sent(e - W)
                piece(gq, j, left_send, g - 2).start()

            piece(gq, j, side_send, side).start()

    def tick(n):
        @pl.loop(0, 2)
        def _(t):
            to_right = jnp.logical_xor(t == 1, own_right)

            @pl.when(to_right)
            def _():
                move_right(n)

            @pl.when(jnp.logical_not(to_right))
            def _():
                move_left(n)

    for n in range(W):
        send_own(n)

    @pl.loop(0, NT)
    def _(j):
        own_piece(j, side_send, side).start()

    stride = max(1, blocks // max(1, NT - W))
    early = blocks // stride
    early = min(early, NT)

    own_copy.wait()

    @pl.loop(0, NS)
    def _(j):
        rows = pl.ds(pl.multiple_of(j * R, R), R)
        qown[rows, :] = unit(qown[rows, :])

    def own_block(b, carry):
        total, pos = carry
        passage_copy(b).wait()
        pun[b] = unit(pun[b])
        st = scores(pun[b], qown[...])
        row = lax.broadcasted_iota(jnp.int32, st.shape, 0)
        live = row < counts[b]
        total = total + jnp.sum(jnp.where(live, jnp.exp(st), 0.0), axis=0, keepdims=True)
        hit = row + b * BR == positive[...].reshape(1, QG)
        pos = pos + jnp.sum(jnp.where(hit, st, 0.0), axis=0, keepdims=True)

        @pl.when(jnp.logical_and(b % stride == stride - 1, b // stride < early))
        def _():
            tick(b // stride)

        return total, pos

    zero = jnp.zeros((1, QG), jnp.float32)
    local_total, pos = lax.fori_loop(0, blocks, own_block, (zero, zero))
    tot_in[g, 0:1, :] = local_total

    for k in range(1, G):
        want_arrival(k).wait_recv()
    wants_in[g] = wants_out[...]
    to_smem = pltpu.make_async_copy(wants_in, wants_s, smem_sem)
    to_smem.start()
    to_smem.wait()
    me = g * REP + r

    @pl.loop(0, G)
    def _(gq):
        found = jnp.int32(0)
        first = jnp.int32(0)
        second = jnp.int32(0)
        for i in range(listed):
            w = wants_s[gq, 0, i]
            local = w - me * blocks
            mine = jnp.logical_and(local >= 0, local < blocks)
            first = jnp.where(jnp.logical_and(mine, found == 0), local, first)
            second = jnp.where(jnp.logical_and(mine, found == 1), local, second)
            found = found + mine.astype(jnp.int32)
        table[gq, 0] = first
        table[gq, 1] = jnp.where(found > 0, counts[first], 0)
        table[gq, 2] = second
        table[gq, 3] = jnp.where(found > 1, counts[second], 0)

    def blk_copy(t):
        slot = t // 2
        cq = t % 2
        return pltpu.make_async_remote_copy(
            blk_out.at[cq, slot],
            blk_in.at[c, slot],
            blk_send.at[cq, slot],
            blk_recv.at[c, slot],
            device_id={"grp": 2 * inner_z + cq},
            device_id_type=MESH,
        )

    def live_copy(cq):
        return pltpu.make_async_remote_copy(
            live_out.at[cq],
            live_in.at[c],
            live_send.at[cq],
            live_recv.at[c],
            device_id={"grp": 2 * inner_z + cq},
            device_id_type=MESH,
        )

    def blk_arrival(t):
        slot = t // 2
        co = t % 2
        return pltpu.make_async_remote_copy(
            blk_out.at[co, slot],
            blk_in.at[co, slot],
            blk_send.at[co, slot],
            blk_recv.at[co, slot],
            device_id={"grp": 2 * end_z + co},
            device_id_type=MESH,
        )

    def live_arrival(co):
        return pltpu.make_async_remote_copy(
            live_out.at[co],
            live_in.at[co],
            live_send.at[co],
            live_recv.at[co],
            device_id={"grp": 2 * end_z + co},
            device_id_type=MESH,
        )

    @pl.when(at_end)
    def _():
        @pl.loop(0, 4)
        def _(t):
            slot = t // 2
            cq = t % 2
            gq = 2 * inner_z + cq
            blk_out[cq, slot] = pun[table[gq, 2 * slot]]
            live_out[cq, slot] = jnp.full((8, QG), table[gq, 2 * slot + 1], jnp.int32)

        @pl.loop(0, 2)
        def _(cq):
            live_copy(cq).start()

        @pl.loop(0, 4)
        def _(t):
            blk_copy(t).start()

    def tot_copy(gq):
        return pltpu.make_async_remote_copy(
            tot_out.at[gq],
            tot_in.at[g],
            tot_send.at[gq],
            tot_recv.at[g],
            device_id={"grp": gq},
            device_id_type=MESH,
        )

    def tot_arrival(src):
        return pltpu.make_async_remote_copy(
            tot_out.at[src],
            tot_in.at[src],
            tot_send.at[src],
            tot_recv.at[src],
            device_id={"grp": src},
            device_id_type=MESH,
        )

    def hard(gq, j):
        rows = pl.ds(pl.multiple_of(j * R, R), R)
        qsub[...] = unit(qall[gq, rows, :])
        total = jnp.zeros((1, R), jnp.float32)
        for slot in range(2):
            st = scores(pun[table[gq, 2 * slot]], qsub[...])
            row = lax.broadcasted_iota(jnp.int32, st.shape, 0)
            live = row < table[gq, 2 * slot + 1]
            total = total + jnp.sum(jnp.where(live, jnp.exp(st), 0.0), axis=0, keepdims=True)
        tot_out[gq, 0:1, rows] = total

        @pl.when(j == NS - 1)
        def _():
            tot_copy(gq).start()

    def compute(n):
        e_right = n + right_skip
        e_left = n + left_skip

        @pl.loop(0, 4)
        def _(t):
            is_left = t % 2 == 0
            e = jnp.where(is_left, e_right, e_left)
            zq = jnp.where(is_left, z - e // NT, z + e // NT)
            j = e % NT
            there = jnp.logical_or(
                jnp.logical_and(is_left, comes_from_left(e)),
                jnp.logical_and(t % 2 == 1, comes_from_right(e)),
            )
            gq = 2 * zq + jnp.where(t < 2, c, 1 - c)

            @pl.when(there)
            def _():
                @pl.when(t >= 2)
                def _():
                    piece(gq, j, side_send, g).wait_recv()

                @pl.when(j % per == per - 1)
                def _():
                    hard(gq, j // per)

    @pl.loop(early, C * NT + early)
    def _(n):
        @pl.when(n < C * NT)
        def _():
            tick(n)

        caught_up = n >= 2 * early
        first = jnp.where(caught_up, n, 2 * (n - early))
        last = jnp.where(caught_up, n, first + 1)

        @pl.loop(first, last + 1)
        def _(m):
            @pl.when(m < C * NT)
            def _():
                compute(m)

        j = n - 2 * early

        @pl.when(jnp.logical_and(j >= 0, j < NS))
        def _():
            for i in range(per):
                piece(side, j * per + i, side_send, g).wait_recv()
            hard(side, j)

    @pl.when(by_end)
    def _():
        @pl.loop(0, 2)
        def _(co):
            live_arrival(co).wait_recv()
            tot_in[2 * end_z + co] = jnp.zeros((8, QG), jnp.float32)

        @pl.loop(0, 4)
        def _(t):
            slot = t // 2
            co = t % 2
            blk_arrival(t).wait_recv()
            st = scores(blk_in[co, slot], qown[...])
            row = lax.broadcasted_iota(jnp.int32, st.shape, 0)
            live = row < live_in[co, slot, 0:1, :]
            tot_in[2 * end_z + co, 0:1, :] += jnp.sum(
                jnp.where(live, jnp.exp(st), 0.0), axis=0, keepdims=True
            )

    @pl.loop(1, G)
    def _(k):
        src = lax.rem(g + k, G)

        @pl.when(jnp.logical_not(by_blocks(src // 2, z)))
        def _():
            tot_arrival(src).wait_recv()

    total = tot_in[0, 0:1, :]
    for k in range(1, G):
        total = total + tot_in[k, 0:1, :]
    loss = jnp.log(total) - pos
    loss_ref[...] = loss.reshape(QG)
    w = weights[...].reshape(1, QG)
    lane = lax.broadcasted_iota(jnp.int32, (8, LANES), 1)
    weighted = jnp.sum(w * loss, axis=1, keepdims=True)
    weight = jnp.sum(w, axis=1, keepdims=True)
    part = jnp.where(lane == 0, weighted, jnp.where(lane == 1, weight, 0.0))

    def exchange(axis, me_, n, out, slots, send, rec):
        def copy(k):
            return pltpu.make_async_remote_copy(
                out,
                slots.at[me_],
                send.at[k],
                rec.at[me_],
                device_id={axis: lax.rem(me_ + k, n)},
                device_id_type=MESH,
            )

        def arrival(k):
            src = lax.rem(me_ + k, n)
            return pltpu.make_async_remote_copy(
                out,
                slots.at[src],
                send.at[k],
                rec.at[src],
                device_id={axis: src},
                device_id_type=MESH,
            )

        for k in range(1, n):
            copy(k).start()
        for k in range(1, n):
            arrival(k).wait_recv()
        for k in range(1, n):
            copy(k).wait_send()

    part_out[...] = part
    part_grp[g] = part
    exchange("grp", g, G, part_out, part_grp, grp_send, grp_recv)
    total = part_grp[0]
    for k in range(1, G):
        total = total + part_grp[k]
    sum_out[...] = total
    part_rep[r] = total
    exchange("rep", r, REP, sum_out, part_rep, rep_send, rep_recv)
    total = part_rep[0]
    for k in range(1, REP):
        total = total + part_rep[k]
    mean_ref[...] = total[0:1, 0:1] / total[0:1, 1:2]

    for k in range(1, G):
        want_copy(k).wait_send()

    @pl.loop(1, G)
    def _(k):
        dst = lax.rem(g + k, G)

        @pl.when(jnp.logical_not(by_blocks(z, dst // 2)))
        def _():
            tot_copy(dst).wait_send()

    @pl.when(at_end)
    def _():
        @pl.loop(0, 2)
        def _(cq):
            live_copy(cq).wait_send()

        @pl.loop(0, 4)
        def _(t):
            blk_copy(t).wait_send()

    @pl.loop(0, NT)
    def _(j):
        own_piece(j, side_send, side).wait_send()

    @pl.loop(0, C * NT)
    def _(n):
        e_right = n + right_skip
        e_left = n + left_skip

        @pl.when(comes_from_left(e_right))
        def _():
            piece(2 * (z - e_right // NT) + c, e_right % NT, side_send, side).wait_send()

        @pl.when(comes_from_right(e_left))
        def _():
            piece(2 * (z + e_left // NT) + c, e_left % NT, side_send, side).wait_send()

    @pl.loop(0, C * NT)
    def _(e):
        @pl.when(jnp.logical_not(goes_right(e + W)))
        def _():
            right_sent(e)

        @pl.when(jnp.logical_not(goes_left(e + W)))
        def _():
            left_sent(e)


def local(G, REP, queries, passages, counts, positive, neg, weights):
    QG, D = queries.shape
    blocks = counts.shape[0]
    BR = passages.shape[0] // blocks
    NT = QG // (PIECE if LANES % PIECE == 0 else LANES)
    dma = pltpu.SemaphoreType.DMA
    vmem = pl.BlockSpec(memory_space=pltpu.VMEM)
    smem = pl.BlockSpec(memory_space=pltpu.SMEM)
    hbm = pl.BlockSpec(memory_space=pl.ANY)
    loss, mean = pl.pallas_call(
        functools.partial(kernel, G, REP),
        out_shape=(
            jax.ShapeDtypeStruct((QG,), jnp.float32),
            jax.ShapeDtypeStruct((1, 1), jnp.float32),
        ),
        in_specs=[smem, vmem, vmem, vmem, hbm, hbm],
        out_specs=(vmem, vmem),
        scratch_shapes=[
            pltpu.VMEM((G, QG, D), jnp.bfloat16),
            pltpu.VMEM((blocks, BR, D), jnp.bfloat16),
            pltpu.VMEM((QG, D), jnp.bfloat16),
            pltpu.VMEM((LANES, D), jnp.bfloat16),
            pltpu.VMEM((8, LANES), jnp.int32),
            pltpu.VMEM((G, 8, LANES), jnp.int32),
            pltpu.SMEM((G, 8, LANES), jnp.int32),
            pltpu.SMEM((G, 4), jnp.int32),
            pltpu.VMEM((G, 8, QG), jnp.float32),
            pltpu.VMEM((G, 8, QG), jnp.float32),
            pltpu.VMEM((8, LANES), jnp.float32),
            pltpu.VMEM((G, 8, LANES), jnp.float32),
            pltpu.VMEM((8, LANES), jnp.float32),
            pltpu.VMEM((REP, 8, LANES), jnp.float32),
            pltpu.VMEM((2, 2, BR, D), jnp.bfloat16),
            pltpu.VMEM((2, 2, BR, D), jnp.bfloat16),
            pltpu.VMEM((2, 2, 8, QG), jnp.int32),
            pltpu.VMEM((2, 2, 8, QG), jnp.int32),
            dma,
            dma((blocks,)),
            dma((G,)),
            dma((G,)),
            dma,
            dma((G, NT)),
            dma((G, NT)),
            dma((G, NT)),
            dma((G, NT)),
            dma((G,)),
            dma((G,)),
            dma((G,)),
            dma((G,)),
            dma((REP,)),
            dma((REP,)),
            dma((2, 2)),
            dma((2, 2)),
            dma((2,)),
            dma((2,)),
        ],
        compiler_params=pltpu.CompilerParams(
            collective_id=0, has_side_effects=True, vmem_limit_bytes=62 * 1024 * 1024
        ),
    )(
        counts,
        neg,
        positive,
        weights,
        queries,
        passages.reshape(blocks, BR, D),
    )
    return loss, mean.reshape(())


def solution(mesh):
    split = P(("grp", "rep"))
    rows = P(("grp", "rep"), None)
    return jax.shard_map(
        functools.partial(local, mesh.shape["grp"], mesh.shape["rep"]),
        mesh=mesh,
        in_specs=(rows, rows, split, split, rows, split),
        out_specs=(split, P()),
        check_vma=False,
    )
```
